32 devices in a mesh: grp: 2 (over y), slc: 4 (over z), coil: 2 (over x), vol: 2 (over core).
Axes of the slice: x: 2, y: 2, z: 4, core: 2. Of those that a mesh axis runs over, the one named last changes fastest.
Arguments:
- images: bfloat16 [4, 32, 2, 220, 220], P(('grp', 'vol'), 'slc'), parts along dimension 0, may hold values from -6 to 6
- coil_maps: bfloat16 [8, 32, 2, 220, 220], P(('grp', 'coil'), 'slc'), parts along dimension 0, may hold values from -3 to 3
- kspace: bfloat16 [4, 4, 4, 2, 220, 220], P(('grp', 'vol'), 'slc', 'coil'), parts along dimension 0, may hold values from -12 to 12
- shift_index: int32 [32], P('slc'), may hold values from 0 to 7
- phase_offset: float32 [32, 220], P('slc'), may hold values from -3.140625 to 3.140625
- group_order: int32 [4], replicated, may hold values from 0 to 3, each once
Outputs:
- grad_phase: float32 [64, 220], P(('grp', 'slc')), parts along dimension 0
The draws below stay inside these ranges and needn't reach their ends.
There are 2 independent parts, one for each index of `grp`. The reference program is written for one: setup_inputs(seed, part) draws one part's arguments, and reference() takes and returns one part's arrays. A program takes and returns all parts, laid end to end along the dimension named above; an argument that names none is the same for every part. Nothing has to cross between parts.
Inputs may be any that keep to these rules, and one draw needn't show every extreme that they name: group_order names each of the 4 measured rows exactly once.
All inputs are finite; a program needn't handle non-finite values.
Results may differ from the reference program's by a relative error of at most 0.0096.
Values may be sent and summed in bfloat16 or wider, within the bound.
A program may use at most 64 MiB of HBM per device.

```python
import math
import jax
import jax.numpy as jnp
from jax import lax

MATRIX = 220
MB = 8
COILS = 4
VOLS = 2
SLICES = 32
GROUPS = 4


def set_ends(drawn, key, low, largest):
    extent = drawn.shape
    place = [jax.random.randint(jax.random.fold_in(key, axis), (), 0, extent[axis]) for axis in range(len(extent))]
    drawn = drawn.at[tuple(place)].set(low)
    longest = extent.index(max(extent))
    place[longest] = (place[longest] + 1) % extent[longest]
    return drawn.at[tuple(place)].set(largest)


def level_of(rng, extent, split, low, largest):
    factor_of, own = 1.0, jax.random.fold_in(rng, 6)
    for position, blocks in split:
        steps = jnp.exp(jax.random.uniform(jax.random.fold_in(own, position), (blocks,), jnp.float32, low / len(split), largest / len(split)))
        factor_of = factor_of * jnp.repeat(steps, extent[position] // blocks).reshape([-1 if axis == position else 1 for axis in range(len(extent))])
    return factor_of


def centred(stream_key, shape, spread, bound, pieces=(), held_as=jnp.bfloat16):
    drawn = jax.random.normal(stream_key, shape, jnp.float32) * spread
    if len(pieces) > 0:
        drawn = level_of(stream_key, shape, pieces, -0.22, 0.18) * drawn
    return jnp.clip(drawn, min=-bound, max=bound).astype(held_as)


def setup_inputs(seed: int = 0, part: int = 0) -> dict:
    seeds = jax.random.split(jax.random.key(seed), 7)
    own_keys = jax.random.split(jax.random.fold_in(seeds[6], part), 7)
    return {
        "images": centred(own_keys[0], (VOLS, SLICES, 2, MATRIX, MATRIX), 1.0, 6.0, ((0, 2), (1, 4))),
        "coil_maps": centred(own_keys[1], (COILS, SLICES, 2, MATRIX, MATRIX), 0.5, 3.0, ((0, 2), (1, 4))),
        "kspace": centred(own_keys[2], (VOLS, GROUPS, COILS, 2, MATRIX, MATRIX), 2.0, 12.0, ((0, 2), (1, 4), (2, 2))),
        "shift_index": set_ends(jax.random.randint(seeds[3], (SLICES,), 0, MB), jax.random.fold_in(seeds[3], 1), 0, MB - 1).astype(jnp.int32),
        "phase_offset": jnp.clip(jax.random.uniform(seeds[4], (SLICES, MATRIX), jnp.float32, -3.140625, 3.140625), -3.140625, 3.140625),
        "group_order": jax.random.permutation(seeds[5], GROUPS).astype(jnp.int32),
    }


def to_half(values):
    return lax.optimization_barrier(values.astype(jnp.bfloat16)).astype(jnp.float32)

def fourier_tables(length):
    positions = jnp.arange(length, dtype=jnp.int32)
    product = positions[:, None] * positions[None, :] % length
    radians = 2.0 * math.pi / length * product.astype(jnp.float32)
    factor = 1.0 / math.sqrt(length)
    return ((jnp.cos(radians) * factor).astype(jnp.bfloat16), (-jnp.sin(radians) * factor).astype(jnp.bfloat16))

def slice_phases(shift_index, phase_offset, length):
    lines = (jnp.arange(length, dtype=jnp.int32) - length // 2).astype(jnp.float32)
    return 2.0 * math.pi / MB * (shift_index.astype(jnp.float32)[:, None] * lines[None, :]) + phase_offset

def reference(images, coil_maps, kspace, shift_index, phase_offset, group_order):
    hp = lax.Precision.HIGHEST
    cos_table, sin_table = fourier_tables(MATRIX)
    cos_full = cos_table.astype(jnp.float32)
    sin_full = sin_table.astype(jnp.float32)
    phase_angle = slice_phases(shift_index, phase_offset, MATRIX)
    cosine = jnp.cos(phase_angle)[None, :, :, None]
    sine = jnp.sin(phase_angle)[None, :, :, None]
    classes = jnp.arange(SLICES, dtype=jnp.int32) % GROUPS
    target = group_order[classes]
    onehot = (target[None, :] == jnp.arange(GROUPS, dtype=jnp.int32)[:, None]).astype(jnp.float32)
    image_re = images[:, :, 0].astype(jnp.float32)
    image_im = images[:, :, 1].astype(jnp.float32)

    def per_coil(packed):
        coil_map, measured = packed
        map_re = coil_map[:, 0].astype(jnp.float32)[None]
        map_im = coil_map[:, 1].astype(jnp.float32)[None]
        coil_re = to_half(map_re * image_re - map_im * image_im)
        coil_im = to_half(map_re * image_im + map_im * image_re)
        half_re = to_half(jnp.einsum('ky,vsyx->vskx', cos_full, coil_re, precision=hp) - jnp.einsum('ky,vsyx->vskx', sin_full, coil_im, precision=hp))
        half_im = to_half(jnp.einsum('ky,vsyx->vskx', cos_full, coil_im, precision=hp) + jnp.einsum('ky,vsyx->vskx', sin_full, coil_re, precision=hp))
        spec_re = jnp.einsum('vsyx,kx->vsyk', half_re, cos_full, precision=hp) - jnp.einsum('vsyx,kx->vsyk', half_im, sin_full, precision=hp)
        spec_im = jnp.einsum('vsyx,kx->vsyk', half_re, sin_full, precision=hp) + jnp.einsum('vsyx,kx->vsyk', half_im, cos_full, precision=hp)
        shift_re = to_half(spec_re * cosine - spec_im * sine)
        shift_im = to_half(spec_re * sine + spec_im * cosine)
        alias_re = jnp.einsum('gs,vsyx->vgyx', onehot, shift_re, precision=hp)
        alias_im = jnp.einsum('gs,vsyx->vgyx', onehot, shift_im, precision=hp)
        resid_re = to_half(alias_re - measured[:, :, 0].astype(jnp.float32))
        resid_im = to_half(alias_im - measured[:, :, 1].astype(jnp.float32))
        chosen_re = resid_re[:, target]
        chosen_im = resid_im[:, target]
        return lax.optimization_barrier(jnp.sum(chosen_im * shift_re - chosen_re * shift_im, axis=(0, 3)))
    per_coil_grad = lax.map(per_coil, (coil_maps, jnp.moveaxis(kspace, 2, 0)))
    return lax.optimization_barrier(jnp.sum(per_coil_grad, axis=0)) * (1.0 / (COILS * VOLS))
```

```python
import functools
import math

import jax
import jax.numpy as jnp
import numpy as np
from jax import lax
from jax.experimental import pallas as pl
from jax.experimental.pallas import tpu as pltpu
from jax.sharding import PartitionSpec as P

MB = 8


def fourier_tables(length):
    positions = jnp.arange(length, dtype=jnp.int32)
    product = positions[:, None] * positions[None, :] % length
    radians = 2.0 * math.pi / length * product.astype(jnp.float32)
    factor = 1.0 / math.sqrt(length)
    return (
        (jnp.cos(radians) * factor).astype(jnp.bfloat16),
        (-jnp.sin(radians) * factor).astype(jnp.bfloat16),
    )


def slice_phases(shift_index, phase_offset, length):
    lines = (jnp.arange(length, dtype=jnp.int32) - length // 2).astype(jnp.float32)
    return (
        2.0 * math.pi / MB * (shift_index.astype(jnp.float32)[:, None] * lines[None, :])
        + phase_offset
    )


ROWS = 32
LAG = 3
PACE = 2
AHEAD = 2
MESH = pl.DeviceIdType.MESH
F32 = jnp.float32
BF16 = jnp.bfloat16


def round_up(value, unit):
    return -(-value // unit) * unit


def static_tables(length):
    positions = np.arange(length, dtype=np.int32)
    product = positions[:, None] * positions[None, :] % length
    radians = np.float32(2.0 * math.pi / length) * product.astype(np.float32)
    factor = np.float32(1.0 / math.sqrt(length))
    table = np.zeros((2, round_up(length, ROWS), length), np.float32)
    table[0, :length] = (np.cos(radians) * factor).astype(jnp.bfloat16)
    table[1, :length] = (-np.sin(radians) * factor).astype(jnp.bfloat16)
    return table.astype(jnp.bfloat16)


def kernel(
    sizes,
    order_hbm,
    shift_hbm,
    offset_hbm,
    table_hbm,
    kspace_hbm,
    images_hbm,
    maps_hbm,
    out_ref,
    order_ref,
    shift_ref,
    offset_ref,
    table_ref,
    kspace_ref,
    image_ref,
    maps_ref,
    trig_ref,
    target,
    turned,
    own,
    to_right,
    to_left,
    from_left,
    from_right,
    columns,
    shares,
    small_sems,
    image_sems,
    maps_sems,
    right_send,
    left_send,
    left_recv,
    right_recv,
    share_send,
    share_recv,
):
    groups, coil_axis, vol_axis = sizes
    per_device, length = image_ref.shape[0], image_ref.shape[-1]
    coils = maps_ref.shape[0]
    rows = table_ref.shape[1]
    spread = per_device // groups
    parts = rows // ROWS
    total = groups * parts
    spot = lax.axis_index("slc")
    coil_at, vol_at = lax.axis_index("coil"), lax.axis_index("vol")
    has_left, has_right = spot > 0, spot < groups - 1
    inner = has_left & has_right
    peers = coil_axis * vol_axis
    mine = coil_at * vol_axis + vol_at

    def peer(distance):
        other = lax.rem(mine + distance, peers)
        return {"coil": other // vol_axis, "vol": lax.rem(other, vol_axis)}

    small = [
        pltpu.make_async_copy(source, target_ref, small_sems.at[which])
        for which, (source, target_ref) in enumerate(
            (
                (table_hbm, table_ref),
                (offset_hbm, offset_ref),
                (shift_hbm, shift_ref),
                (order_hbm, order_ref),
                (kspace_hbm.at[0, 0], kspace_ref),
            )
        )
    ]

    def slice_of(piece):
        return piece // spread + lax.rem(piece, spread) * groups

    def image_copy(piece):
        at = slice_of(piece)
        return pltpu.make_async_copy(
            images_hbm.at[0, at], image_ref.at[at], image_sems.at[piece]
        )

    def maps_copy(piece, coil):
        at = slice_of(piece)
        return pltpu.make_async_copy(
            maps_hbm.at[coil, at], maps_ref.at[coil, at], maps_sems.at[piece, coil]
        )

    def fetch(piece):
        image_copy(piece).start()
        for coil in range(coils):
            maps_copy(piece, coil).start()

    for copy in small:
        copy.start()
    for piece in range(min(AHEAD, per_device)):
        fetch(piece)

    barrier = pltpu.get_barrier_semaphore()

    @pl.when(has_left)
    def _():
        pl.semaphore_signal(barrier, inc=1, device_id={"slc": spot - 1}, device_id_type=MESH)

    @pl.when(has_right)
    def _():
        pl.semaphore_signal(barrier, inc=1, device_id={"slc": spot + 1}, device_id_type=MESH)

    for distance in range(1, peers):
        pl.semaphore_signal(barrier, inc=1, device_id=peer(distance), device_id_type=MESH)

    def right_copy(chunk):
        return pltpu.make_async_remote_copy(
            src_ref=to_right.at[chunk],
            dst_ref=from_left.at[chunk],
            send_sem=right_send.at[chunk],
            recv_sem=left_recv.at[chunk],
            device_id={"slc": spot + 1},
            device_id_type=MESH,
        )

    def left_copy(chunk):
        return pltpu.make_async_remote_copy(
            src_ref=to_left.at[chunk],
            dst_ref=from_right.at[chunk],
            send_sem=left_send.at[chunk],
            recv_sem=right_recv.at[chunk],
            device_id={"slc": spot - 1},
            device_id_type=MESH,
        )

    columns[...] = jnp.zeros_like(columns)
    trig_ref[...] = jnp.zeros_like(trig_ref)
    target[...] = jnp.zeros_like(target)

    def dot(left, right):
        return jnp.dot(left, right, preferred_element_type=F32)

    def planes(ref):
        pair = jnp.swapaxes(ref[...].astype(F32), 0, 1)
        return pair[0], pair[1]

    for copy in small:
        copy.wait()

    row_at = lax.broadcasted_iota(jnp.int32, (per_device, length), 0)
    line_at = lax.broadcasted_iota(jnp.int32, (per_device, length), 1) - length // 2
    shift = jnp.zeros((per_device, length), jnp.int32)
    for at in range(per_device):
        shift = jnp.where(row_at == at, shift_ref[at], shift)
    eighths = (shift * line_at) & (MB - 1)
    angle = 2.0 * math.pi / MB * eighths.astype(F32) + offset_ref[...]
    trig_ref[0, :length, :per_device] = jnp.cos(angle).T
    trig_ref[1, :length, :per_device] = jnp.sin(angle).T

    straight, across = table_ref[0, :length], table_ref[1, :length]
    real_part = jnp.concatenate([straight, -across], axis=1)
    imaginary_part = jnp.concatenate([across, straight], axis=1)
    pulled = []
    for coil in range(coils):
        seen_re, seen_im = planes(kspace_ref.at[coil])
        pulled.append(
            dot(seen_re.astype(BF16), real_part) + dot(seen_im.astype(BF16), imaginary_part)
        )
    target[:length] = jnp.concatenate(pulled, axis=1)

    def compute(piece):
        within, group = slice_of(piece), piece // spread
        image_copy(piece).wait()
        for coil in range(coils):
            maps_copy(piece, coil).wait()

        @pl.when(piece + AHEAD < per_device)
        def _():
            fetch(piece + AHEAD)

        lane = lax.broadcasted_iota(jnp.int32, trig_ref.shape[1:], 1)
        cosine = jnp.sum(jnp.where(lane == within, trig_ref[0], 0.0), axis=1, keepdims=True)
        sine = jnp.sum(jnp.where(lane == within, trig_ref[1], 0.0), axis=1, keepdims=True)
        cos_table, sin_table = table_ref[0].astype(F32), table_ref[1].astype(F32)
        phased_re = cos_table * cosine - sin_table * sine
        phased_im = cos_table * sine + sin_table * cosine
        first = jnp.concatenate([phased_re, -phased_im], axis=0).astype(BF16)
        second = jnp.concatenate([phased_im, phased_re], axis=0).astype(BF16)
        image_re, image_im = planes(image_ref.at[within])
        plain, crossed = [], []
        for coil in range(coils):
            map_re, map_im = planes(maps_ref.at[coil, within])
            coil_re = (map_re * image_re - map_im * image_im).astype(BF16)
            coil_im = (map_re * image_im + map_im * image_re).astype(BF16)
            plain += [coil_re, coil_im]
            crossed += [-coil_im, coil_re]
        both = dot(first, jnp.concatenate(plain, axis=1)) + dot(
            second, jnp.concatenate(crossed, axis=1)
        )
        turned[within] = both[rows:].astype(BF16)
        span = pl.ds(group * parts, parts)
        value = both[:rows]
        if spread == 1:
            opening = True
        else:
            opening = lax.rem(piece, spread) == 0
        held = jnp.where(order_ref[group] == spot, F32(1.0), F32(0.0))

        def store(fresh):
            own[span] = fresh.reshape(parts, ROWS, -1)

        if spread == 1:
            store(value - held * target[...])
        else:

            @pl.when(opening)
            def _():
                store(value - held * target[...])

            @pl.when(jnp.logical_not(opening))
            def _():
                store(value + own[span].reshape(rows, -1))

    def launch(group):
        @pl.when(jnp.logical_not(has_left))
        def _():
            def send(chunk, carry):
                to_right[chunk] = own[chunk].astype(BF16)
                right_copy(chunk).start()
                return carry

            lax.fori_loop(group * parts, (group + 1) * parts, send, 0)

        @pl.when(jnp.logical_not(has_right))
        def _():
            def send(chunk, carry):
                to_left[chunk] = own[chunk].astype(BF16)
                left_copy(chunk).start()
                return carry

            lax.fori_loop(group * parts, (group + 1) * parts, send, 0)

    skew = 2 * spot - (groups - 1)
    between = jnp.where(inner, LAG, 0)
    late_right = between * jnp.maximum(0, skew)
    late_left = between * jnp.maximum(0, -skew)
    late = late_right + late_left

    def gradient(chunk):
        value = own[chunk]
        value = value + jnp.where(has_left, from_left[chunk].astype(F32), F32(0.0))
        value = value + jnp.where(has_right, from_right[chunk].astype(F32), F32(0.0))
        group = chunk // parts
        at = pl.multiple_of((chunk - group * parts) * ROWS, ROWS)
        lane = lax.broadcasted_iota(jnp.int32, (ROWS, columns.shape[1]), 1)
        block = columns[pl.ds(at, ROWS), :]
        for step in range(spread):
            within = group + step * groups
            product = value * turned[within, pl.ds(at, ROWS), :].astype(F32)
            block = jnp.where(lane == within, jnp.sum(product, axis=1, keepdims=True), block)
        columns[pl.ds(at, ROWS), :] = block

    def wave(tick, carry):
        chunk = tick - late_right

        @pl.when(has_left & (chunk >= 0) & (chunk < total))
        def _():
            right_copy(chunk).wait_recv()

            @pl.when(has_right)
            def _():
                to_right[chunk] = (from_left[chunk].astype(F32) + own[chunk]).astype(BF16)
                right_copy(chunk).start()

        other = tick - late_left

        @pl.when(has_right & (other >= 0) & (other < total))
        def _():
            left_copy(other).wait_recv()

            @pl.when(has_left)
            def _():
                to_left[other] = (from_right[other].astype(F32) + own[other]).astype(BF16)
                left_copy(other).start()

        done = tick - late

        @pl.when(done >= 0)
        def _():
            gradient(done)

        return carry

    def upto(piece):
        ready = (piece // spread) * parts
        wanted = jnp.minimum(jnp.maximum(0, PACE * (piece - spread - 1)), ready)
        return jnp.where(inner, wanted, 0)

    arrivals = has_left.astype(jnp.int32) + has_right.astype(jnp.int32) + (peers - 1)
    pl.semaphore_wait(barrier, arrivals)

    def advance(piece, carry):
        compute(piece)

        @pl.when(lax.rem(piece, spread) == spread - 1)
        def _():
            launch(piece // spread)

        lax.fori_loop(upto(piece), upto(piece + 1), wave, 0)
        return carry

    lax.fori_loop(0, per_device, advance, 0)
    lax.fori_loop(upto(per_device), total + late, wave, 0)

    shares[mine] = columns[...].T[:per_device]

    def share_copy(distance):
        return pltpu.make_async_remote_copy(
            src_ref=shares.at[mine],
            dst_ref=shares.at[mine],
            send_sem=share_send.at[distance],
            recv_sem=share_recv.at[distance],
            device_id=peer(distance),
            device_id_type=MESH,
        )

    for distance in range(1, peers):
        share_copy(distance).start()

    @pl.when(has_right)
    def _():
        def done(chunk, carry):
            right_copy(chunk).wait_send()
            return carry

        lax.fori_loop(0, total, done, 0)

    @pl.when(has_left)
    def _():
        def done(chunk, carry):
            left_copy(chunk).wait_send()
            return carry

        lax.fori_loop(0, total, done, 0)

    for distance in range(1, peers):
        share_copy(distance).wait()
    result = shares[0]
    for other in range(1, peers):
        result = result + shares[other]
    out_ref[...] = result[:, :length] * (1.0 / (coils * peers))


def fused(images, coil_maps, kspace, shift_index, phase_offset, group_order):
    per_device, length = images.shape[1], images.shape[-1]
    coils = coil_maps.shape[0]
    groups = lax.axis_size("slc")
    sizes = (groups, lax.axis_size("coil"), lax.axis_size("vol"))
    peers = sizes[1] * sizes[2]
    table = static_tables(length)
    rows, wide = table.shape[1], round_up(length, 128)
    width = coils * 2 * length
    chunks = groups * rows // ROWS
    anywhere = pl.BlockSpec(memory_space=pl.ANY)
    block = pltpu.VMEM((chunks, ROWS, width), BF16)
    side = pltpu.SemaphoreType.DMA((chunks,))
    return pl.pallas_call(
        functools.partial(kernel, sizes),
        out_shape=jax.ShapeDtypeStruct((per_device, length), F32),
        in_specs=[anywhere] * 7,
        out_specs=pl.BlockSpec(memory_space=pltpu.VMEM),
        scratch_shapes=[
            pltpu.SMEM(group_order.shape, jnp.int32),
            pltpu.SMEM(shift_index.shape, jnp.int32),
            pltpu.VMEM((per_device, length), F32),
            pltpu.VMEM(table.shape, BF16),
            pltpu.VMEM((coils, length, 2, length), BF16),
            pltpu.VMEM((per_device, length, 2, length), BF16),
            pltpu.VMEM((coils, per_device, length, 2, length), BF16),
            pltpu.VMEM((2, rows, 128), F32),
            pltpu.VMEM((rows, width), F32),
            pltpu.VMEM((per_device, rows, width), BF16),
            pltpu.VMEM((chunks, ROWS, width), F32),
            block,
            block,
            block,
            block,
            pltpu.VMEM((wide, 128), F32),
            pltpu.VMEM((peers, per_device, wide), F32),
            pltpu.SemaphoreType.DMA((5,)),
            pltpu.SemaphoreType.DMA((per_device,)),
            pltpu.SemaphoreType.DMA((per_device, coils)),
            side,
            side,
            side,
            side,
            pltpu.SemaphoreType.DMA((peers,)),
            pltpu.SemaphoreType.DMA((peers,)),
        ],
        compiler_params=pltpu.CompilerParams(
            collective_id=0, has_side_effects=True, vmem_limit_bytes=60 * 2**20
        ),
    )(
        group_order,
        shift_index,
        phase_offset,
        jnp.asarray(table),
        jnp.swapaxes(kspace, 3, 4),
        jnp.swapaxes(images, 2, 3),
        jnp.swapaxes(coil_maps, 2, 3),
    )


def program(images, coil_maps, kspace, shift_index, phase_offset, group_order):
    arguments = (images, coil_maps, kspace, shift_index, phase_offset, group_order)
    groups = lax.axis_size("slc")
    even = images.shape[1] % groups == 0 and images.shape[0] == 1 and kspace.shape[1] == 1
    if even and images.shape[1] <= 128 and groups > 2:
        return fused(*arguments)
    return body(*arguments)


def body(images, coil_maps, kspace, shift_index, phase_offset, group_order):
    per_device = images.shape[1]
    matrix = images.shape[-1]
    groups = lax.axis_size("slc")
    spread = max(1, per_device // groups)
    slot_count = groups * spread
    cos_table, sin_table = fourier_tables(matrix)
    section_one = jnp.stack([jnp.stack([cos_table, -sin_table]), jnp.stack([sin_table, cos_table])])
    section_two = jnp.stack([jnp.stack([cos_table, sin_table]), jnp.stack([-sin_table, cos_table])])
    image_re = images[:, None, :, 0].astype(jnp.float32)
    image_im = images[:, None, :, 1].astype(jnp.float32)
    map_re = coil_maps[None, :, :, 0].astype(jnp.float32)
    map_im = coil_maps[None, :, :, 1].astype(jnp.float32)
    coil_image = jnp.stack(
        [map_re * image_re - map_im * image_im, map_re * image_im + map_im * image_re], axis=3
    ).astype(jnp.bfloat16)
    partly = jnp.einsum(
        "pqky,tcsqyx->tcspkx", section_one, coil_image, preferred_element_type=jnp.float32
    ).astype(jnp.bfloat16)
    spectra = jnp.einsum(
        "tcsqyx,qpkx->tcspyk", partly, section_two, preferred_element_type=jnp.float32
    )
    phase_angle = slice_phases(shift_index, phase_offset, matrix)
    cosine = jnp.cos(phase_angle)[None, None, :, :, None]
    sine = jnp.sin(phase_angle)[None, None, :, :, None]
    spec_re = spectra[:, :, :, 0]
    spec_im = spectra[:, :, :, 1]
    shifted = jnp.stack(
        [spec_re * cosine - spec_im * sine, spec_re * sine + spec_im * cosine], axis=3
    ).astype(jnp.bfloat16)
    position = lax.axis_index("slc")
    within = jnp.arange(per_device, dtype=jnp.int32)
    classes = (position * per_device + within) % groups
    class_match = (classes[:, None] == jnp.arange(groups, dtype=jnp.int32)[None, :]).astype(
        jnp.int32
    )
    target = jnp.sum(class_match * group_order[None, :], axis=1)
    slot_index = target * spread + within // groups
    onehot = (jnp.arange(slot_count, dtype=jnp.int32)[:, None] == slot_index[None, :]).astype(
        jnp.int32
    )
    source = jnp.sum(onehot * within[None, :], axis=1)
    filled = jnp.sum(onehot, axis=1)
    outgoing = jnp.take(shifted, source, axis=2)
    outgoing = jnp.where(
        filled[None, None, :, None, None, None] > 0, outgoing, jnp.zeros_like(outgoing)
    )
    incoming = lax.all_to_all(outgoing, "slc", split_axis=2, concat_axis=2, tiled=True)
    aliased = jnp.sum(incoming, axis=2, dtype=jnp.float32)
    residual = (aliased - kspace[:, 0].astype(jnp.float32)).astype(jnp.bfloat16)
    partial_value = jnp.einsum(
        "tcpyx,tcyx->py",
        incoming[:, :, :, 0],
        residual[:, :, 1],
        preferred_element_type=jnp.float32,
    )
    partial_value = partial_value - jnp.einsum(
        "tcpyx,tcyx->py",
        incoming[:, :, :, 1],
        residual[:, :, 0],
        preferred_element_type=jnp.float32,
    )
    returned = lax.all_to_all(partial_value, "slc", split_axis=0, concat_axis=0, tiled=True)
    local_grad = jnp.dot(onehot.T.astype(jnp.float32), returned, precision=lax.Precision.HIGHEST)
    summed = lax.psum(local_grad, "coil")
    summed = lax.psum(summed, "vol")
    factor = 1.0 / (
        coil_maps.shape[0] * lax.axis_size("coil") * images.shape[0] * lax.axis_size("vol")
    )
    return summed * factor


def solution(mesh):
    placed = (
        P(("grp", "vol"), "slc", None, None, None),
        P(("grp", "coil"), "slc", None, None, None),
        P(("grp", "vol"), "slc", "coil", None, None, None),
        P("slc"),
        P("slc", None),
        P(),
    )
    return jax.shard_map(
        program, mesh=mesh, in_specs=placed, out_specs=P(("grp", "slc"), None), check_vma=False
    )
```

```python
import functools
import math

import jax
import jax.numpy as jnp
import numpy as np
from jax import lax
from jax.experimental import pallas as pl
from jax.experimental.pallas import tpu as pltpu
from jax.sharding import PartitionSpec as P

MB = 8


def fourier_tables(length):
    positions = jnp.arange(length, dtype=jnp.int32)
    product = positions[:, None] * positions[None, :] % length
    radians = 2.0 * math.pi / length * product.astype(jnp.float32)
    factor = 1.0 / math.sqrt(length)
    return (
        (jnp.cos(radians) * factor).astype(jnp.bfloat16),
        (-jnp.sin(radians) * factor).astype(jnp.bfloat16),
    )


def slice_phases(shift_index, phase_offset, length):
    lines = (jnp.arange(length, dtype=jnp.int32) - length // 2).astype(jnp.float32)
    return (
        2.0 * math.pi / MB * (shift_index.astype(jnp.float32)[:, None] * lines[None, :])
        + phase_offset
    )


ROWS = 32
LAG = 4
PACE = 2
AHEAD = 2
MESH = pl.DeviceIdType.MESH
F32 = jnp.float32
BF16 = jnp.bfloat16


def round_up(value, unit):
    return -(-value // unit) * unit


def static_tables(length):
    positions = np.arange(length, dtype=np.int32)
    product = positions[:, None] * positions[None, :] % length
    radians = np.float32(2.0 * math.pi / length) * product.astype(np.float32)
    factor = np.float32(1.0 / math.sqrt(length))
    cosine = (np.cos(radians) * factor).astype(jnp.bfloat16)
    sine = (-np.sin(radians) * factor).astype(jnp.bfloat16)
    deep = round_up(length, 128)
    table = np.zeros((2, round_up(length, ROWS), 2 * deep), np.float32)
    table[0, :length, :length], table[0, :length, deep : deep + length] = cosine, sine
    table[1, :length, :length], table[1, :length, deep : deep + length] = -sine, cosine
    return table.astype(jnp.bfloat16)


def kernel(
    sizes,
    order_hbm,
    shift_hbm,
    offset_hbm,
    table_hbm,
    kspace_hbm,
    images_hbm,
    maps_hbm,
    out_ref,
    order_ref,
    shift_ref,
    offset_ref,
    table_ref,
    kspace_ref,
    image_ref,
    maps_ref,
    trig_ref,
    target,
    phased,
    crossing,
    stacked,
    seen,
    stage,
    turned,
    own,
    to_right,
    to_left,
    from_left,
    from_right,
    columns,
    shares,
    small_sems,
    image_sems,
    maps_sems,
    right_send,
    left_send,
    left_recv,
    right_recv,
    share_send,
    share_recv,
):
    groups, coil_axis, vol_axis = sizes
    per_device, length = image_ref.shape[0], image_ref.shape[-1]
    flat = (2 * length, length)
    coils = maps_ref.shape[0]
    rows, deep = table_ref.shape[1], table_ref.shape[2] // 2
    spread = per_device // groups
    parts = rows // ROWS
    total = groups * parts
    spot = lax.axis_index("slc")
    coil_at, vol_at = lax.axis_index("coil"), lax.axis_index("vol")
    has_left, has_right = spot > 0, spot < groups - 1
    inner = has_left & has_right
    peers = coil_axis * vol_axis
    mine = coil_at * vol_axis + vol_at

    def peer(distance):
        other = lax.rem(mine + distance, peers)
        return {"coil": other // vol_axis, "vol": lax.rem(other, vol_axis)}

    small = [
        pltpu.make_async_copy(source, target_ref, small_sems.at[which])
        for which, (source, target_ref) in enumerate(
            (
                (table_hbm, table_ref),
                (offset_hbm, offset_ref),
                (shift_hbm, shift_ref),
                (order_hbm, order_ref),
            )
        )
    ]
    small += [
        pltpu.make_async_copy(
            kspace_hbm.at[0, 0, coil].reshape(flat), kspace_ref.at[coil], small_sems.at[4 + coil]
        )
        for coil in range(coils)
    ]

    def slice_of(piece):
        return piece // spread + lax.rem(piece, spread) * groups

    def image_copy(piece):
        at = slice_of(piece)
        return pltpu.make_async_copy(
            images_hbm.at[0, at].reshape(flat), image_ref.at[at], image_sems.at[piece]
        )

    def maps_copy(piece, coil):
        at = slice_of(piece)
        return pltpu.make_async_copy(
            maps_hbm.at[coil, at].reshape(flat), maps_ref.at[coil, at], maps_sems.at[piece, coil]
        )

    def fetch(piece):
        image_copy(piece).start()
        for coil in range(coils):
            maps_copy(piece, coil).start()

    for copy in small:
        copy.start()
    for piece in range(min(AHEAD, per_device)):
        fetch(piece)

    barrier = pltpu.get_barrier_semaphore()

    @pl.when(has_left)
    def _():
        pl.semaphore_signal(barrier, inc=1, device_id={"slc": spot - 1}, device_id_type=MESH)

    @pl.when(has_right)
    def _():
        pl.semaphore_signal(barrier, inc=1, device_id={"slc": spot + 1}, device_id_type=MESH)

    for distance in range(1, peers):
        pl.semaphore_signal(barrier, inc=1, device_id=peer(distance), device_id_type=MESH)

    def right_copy(chunk):
        return pltpu.make_async_remote_copy(
            src_ref=to_right.at[chunk],
            dst_ref=from_left.at[chunk],
            send_sem=right_send.at[chunk],
            recv_sem=left_recv.at[chunk],
            device_id={"slc": spot + 1},
            device_id_type=MESH,
        )

    def left_copy(chunk):
        return pltpu.make_async_remote_copy(
            src_ref=to_left.at[chunk],
            dst_ref=from_right.at[chunk],
            send_sem=left_send.at[chunk],
            recv_sem=right_recv.at[chunk],
            device_id={"slc": spot - 1},
            device_id_type=MESH,
        )

    columns[...] = jnp.zeros_like(columns)
    trig_ref[...] = jnp.zeros_like(trig_ref)
    target[...] = jnp.zeros_like(target)

    def dot(left, right):
        return jnp.dot(left, right, preferred_element_type=F32)

    blocks = [(low, min(low + ROWS, length)) for low in range(0, length, ROWS)]

    lanes = [(low, min(low + 128, length)) for low in range(0, length, 128)]

    def unfold(slot, ref):
        for tile, (left, right) in enumerate(lanes):
            stage[slot, tile, :, : right - left] = ref[:, left:right].astype(F32)

    def planes(slot, low, high):
        pair = []
        for part in range(2):
            pieces = []
            for tile, (left, right) in enumerate(lanes):
                every = pl.ds(2 * low + part, high - low, stride=2)
                pieces.append(stage[slot, tile, every, :][:, : right - left])
            pair.append(jnp.concatenate(pieces, axis=1))
        return pair

    def side_by_side(parts_of):
        filled = []
        for part in parts_of:
            filled.append(part)
            filled.append(jnp.zeros((part.shape[0], rows - length), part.dtype))
        return jnp.concatenate(filled, axis=1)

    for copy in small:
        copy.wait()

    row_at = lax.broadcasted_iota(jnp.int32, (per_device, length), 0)
    line_at = lax.broadcasted_iota(jnp.int32, (per_device, length), 1) - length // 2
    shift = jnp.zeros((per_device, length), jnp.int32)
    for at in range(per_device):
        shift = jnp.where(row_at == at, shift_ref[at], shift)
    eighths = (shift * line_at) & (MB - 1)
    angle = 2.0 * math.pi / MB * eighths.astype(F32) + offset_ref[...]
    trig_ref[0, :length, :per_device] = jnp.cos(angle).T
    trig_ref[1, :length, :per_device] = jnp.sin(angle).T

    straight = table_ref[0, :length, :length]
    across = table_ref[0, :length, deep : deep + length]
    pulled = []
    for coil in range(coils):
        unfold(coil, kspace_ref.at[coil])
        for low, high in blocks:
            seen_re, seen_im = planes(coil, low, high)
            seen[0, low:high] = seen_re.astype(BF16)
            seen[1, low:high] = seen_im.astype(BF16)
        seen_re, seen_im = seen[0], seen[1]
        pulled.append(dot(seen_re, straight) + dot(seen_im, across))
        pulled.append(dot(seen_im, straight) - dot(seen_re, across))
    target[:length] = side_by_side(pulled)

    def phases(within):
        lane = lax.broadcasted_iota(jnp.int32, trig_ref.shape[1:], 1)
        cosine = jnp.sum(jnp.where(lane == within, trig_ref[0], 0.0), axis=1, keepdims=True)
        sine = jnp.sum(jnp.where(lane == within, trig_ref[1], 0.0), axis=1, keepdims=True)
        return cosine, sine

    def compute(piece):
        within, step = slice_of(piece), lax.rem(piece, spread)
        image_copy(piece).wait()
        for coil in range(coils):
            maps_copy(piece, coil).wait()

        @pl.when(piece + AHEAD < per_device)
        def _():
            fetch(piece + AHEAD)

        cosine, sine = phases(within)
        for low in range(0, rows, ROWS):
            span = slice(low, low + ROWS)
            turn = table_ref[0, span].astype(F32) * cosine[span]
            turn = turn + table_ref[1, span].astype(F32) * sine[span]
            phased[step, span] = turn.astype(BF16)
        edge = length // 16 * 16
        for half in range(2):
            stacked[piece, half * deep + edge : (half + 1) * deep] = jnp.zeros(
                (deep - edge, stacked.shape[2]), BF16
            )
        unfold(coils, image_ref.at[within])
        for coil in range(coils):
            unfold(coil, maps_ref.at[coil, within])
        for low, high in blocks:
            image_re, image_im = planes(coils, low, high)
            plain, crossed = [], []
            for coil in range(coils):
                map_re, map_im = planes(coil, low, high)
                coil_re = (map_re * image_re - map_im * image_im).astype(BF16)
                coil_im = (map_re * image_im + map_im * image_re).astype(BF16)
                plain += [coil_re, coil_im]
                crossed += [-coil_im, coil_re]
            stacked[piece, low:high] = side_by_side(plain)
            stacked[piece, deep + low : deep + high] = side_by_side(crossed)

    def combine(group):
        left = jnp.concatenate([phased[step] for step in range(spread)], axis=1)
        right = stacked[pl.ds(group * spread, spread)].reshape(spread * 2 * deep, -1)
        held = jnp.where(order_ref[group] == spot, F32(1.0), F32(0.0))
        value = dot(left, right) - held * target[...]
        own[pl.ds(group * parts, parts)] = value.reshape(parts, ROWS, -1)

    def rotate(piece):
        within = slice_of(piece)
        cosine, sine = phases(within)
        for low in range(0, rows, ROWS):
            span = slice(low, low + ROWS)
            turn = table_ref[1, span].astype(F32) * cosine[span]
            turn = turn - table_ref[0, span].astype(F32) * sine[span]
            crossing[span] = turn.astype(BF16)
        turned[within] = dot(crossing[...], stacked[piece]).astype(BF16)

    def launch(group):
        @pl.when(jnp.logical_not(has_left))
        def _():
            def send(chunk, carry):
                to_right[chunk] = own[chunk].astype(BF16)
                right_copy(chunk).start()
                return carry

            lax.fori_loop(group * parts, (group + 1) * parts, send, 0)

        @pl.when(jnp.logical_not(has_right))
        def _():
            def send(chunk, carry):
                to_left[chunk] = own[chunk].astype(BF16)
                left_copy(chunk).start()
                return carry

            lax.fori_loop(group * parts, (group + 1) * parts, send, 0)

    skew = 2 * spot - (groups - 1)
    between = jnp.where(inner, LAG, 0)
    late_right = between * jnp.maximum(0, skew)
    late_left = between * jnp.maximum(0, -skew)
    late = late_right + late_left

    def gradient(chunk):
        value = own[chunk]
        value = value + jnp.where(has_left, from_left[chunk].astype(F32), F32(0.0))
        value = value + jnp.where(has_right, from_right[chunk].astype(F32), F32(0.0))
        group = chunk // parts
        at = pl.multiple_of((chunk - group * parts) * ROWS, ROWS)
        lane = lax.broadcasted_iota(jnp.int32, (ROWS, columns.shape[1]), 1)
        block = columns[pl.ds(at, ROWS), :]
        for step in range(spread):
            within = group + step * groups
            product = value * turned[within, pl.ds(at, ROWS), :].astype(F32)
            block = jnp.where(lane == within, jnp.sum(product, axis=1, keepdims=True), block)
        columns[pl.ds(at, ROWS), :] = block

    def wave(tick, carry):
        chunk = tick - late_right

        @pl.when(has_left & (chunk >= 0) & (chunk < total))
        def _():
            right_copy(chunk).wait_recv()

            @pl.when(has_right)
            def _():
                to_right[chunk] = (from_left[chunk].astype(F32) + own[chunk]).astype(BF16)
                right_copy(chunk).start()

        other = tick - late_left

        @pl.when(has_right & (other >= 0) & (other < total))
        def _():
            left_copy(other).wait_recv()

            @pl.when(has_left)
            def _():
                to_left[other] = (from_right[other].astype(F32) + own[other]).astype(BF16)
                left_copy(other).start()

        done = tick - late

        @pl.when(done >= 0)
        def _():
            gradient(done)

        return carry

    def upto(piece):
        ready = (jnp.maximum(piece - 1, 0) // spread) * parts
        wanted = jnp.minimum(jnp.maximum(0, PACE * (piece - spread - 1)), ready)
        return jnp.where(inner, wanted, 0)

    arrivals = has_left.astype(jnp.int32) + has_right.astype(jnp.int32) + (peers - 1)
    pl.semaphore_wait(barrier, arrivals)

    def advance(piece, carry):
        compute(piece)

        @pl.when(lax.rem(piece, spread) == spread - 1)
        def _():
            combine(piece // spread)
            launch(piece // spread)

        @pl.when(piece >= spread - 1)
        def _():
            rotate(piece - (spread - 1))

        lax.fori_loop(upto(piece), upto(piece + 1), wave, 0)
        return carry

    lax.fori_loop(0, per_device, advance, 0)
    for piece in range(per_device - spread + 1, per_device):
        rotate(piece)
    lax.fori_loop(upto(per_device), total + late, wave, 0)

    shares[mine] = columns[...].T[:per_device]

    def share_copy(distance):
        return pltpu.make_async_remote_copy(
            src_ref=shares.at[mine],
            dst_ref=shares.at[mine],
            send_sem=share_send.at[distance],
            recv_sem=share_recv.at[distance],
            device_id=peer(distance),
            device_id_type=MESH,
        )

    for distance in range(1, peers):
        share_copy(distance).start()

    @pl.when(has_right)
    def _():
        def done(chunk, carry):
            right_copy(chunk).wait_send()
            return carry

        lax.fori_loop(0, total, done, 0)

    @pl.when(has_left)
    def _():
        def done(chunk, carry):
            left_copy(chunk).wait_send()
            return carry

        lax.fori_loop(0, total, done, 0)

    for distance in range(1, peers):
        share_copy(distance).wait()
    result = shares[0]
    for other in range(1, peers):
        result = result + shares[other]
    out_ref[...] = result[:, :length]


def fused(images, coil_maps, kspace, shift_index, phase_offset, group_order):
    per_device, length = images.shape[1], images.shape[-1]
    coils = coil_maps.shape[0]
    groups = lax.axis_size("slc")
    sizes = (groups, lax.axis_size("coil"), lax.axis_size("vol"))
    peers = sizes[1] * sizes[2]
    table = static_tables(length)
    rows, wide = table.shape[1], round_up(length, 128)
    width, deep = coils * 2 * rows, table.shape[2] // 2
    spread = per_device // groups
    chunks = groups * rows // ROWS
    anywhere = pl.BlockSpec(memory_space=pl.ANY)
    block = pltpu.VMEM((chunks, ROWS, width), BF16)
    side = pltpu.SemaphoreType.DMA((chunks,))
    summed = pl.pallas_call(
        functools.partial(kernel, sizes),
        out_shape=jax.ShapeDtypeStruct((per_device, length), F32),
        in_specs=[anywhere] * 7,
        out_specs=pl.BlockSpec(memory_space=pltpu.VMEM),
        scratch_shapes=[
            pltpu.SMEM(group_order.shape, jnp.int32),
            pltpu.SMEM(shift_index.shape, jnp.int32),
            pltpu.VMEM((per_device, length), F32),
            pltpu.VMEM(table.shape, BF16),
            pltpu.VMEM((coils, 2 * length, length), BF16),
            pltpu.VMEM((per_device, 2 * length, length), BF16),
            pltpu.VMEM((coils, per_device, 2 * length, length), BF16),
            pltpu.VMEM((2, rows, 128), F32),
            pltpu.VMEM((rows, width), F32),
            pltpu.VMEM((spread, rows, 2 * deep), BF16),
            pltpu.VMEM((rows, 2 * deep), BF16),
            pltpu.VMEM((per_device, 2 * deep, width), BF16),
            pltpu.VMEM((2, length, length), BF16),
            pltpu.VMEM((coils + 1, wide // 128, 2 * length, 128), F32),
            pltpu.VMEM((per_device, rows, width), BF16),
            pltpu.VMEM((chunks, ROWS, width), F32),
            block,
            block,
            block,
            block,
            pltpu.VMEM((wide, 128), F32),
            pltpu.VMEM((peers, per_device, wide), F32),
            pltpu.SemaphoreType.DMA((4 + coils,)),
            pltpu.SemaphoreType.DMA((per_device,)),
            pltpu.SemaphoreType.DMA((per_device, coils)),
            side,
            side,
            side,
            side,
            pltpu.SemaphoreType.DMA((peers,)),
            pltpu.SemaphoreType.DMA((peers,)),
        ],
        compiler_params=pltpu.CompilerParams(
            collective_id=0, has_side_effects=True, vmem_limit_bytes=60 * 2**20
        ),
    )(
        group_order,
        shift_index,
        phase_offset,
        jnp.asarray(table),
        jnp.swapaxes(kspace, 3, 4),
        jnp.swapaxes(images, 2, 3),
        jnp.swapaxes(coil_maps, 2, 3),
    )
    return summed * (1.0 / (coils * peers))


def program(images, coil_maps, kspace, shift_index, phase_offset, group_order):
    arguments = (images, coil_maps, kspace, shift_index, phase_offset, group_order)
    groups = lax.axis_size("slc")
    even = images.shape[1] % groups == 0 and images.shape[0] == 1 and kspace.shape[1] == 1
    if even and images.shape[1] <= 128 and groups > 2:
        return fused(*arguments)
    return body(*arguments)


def body(images, coil_maps, kspace, shift_index, phase_offset, group_order):
    per_device = images.shape[1]
    matrix = images.shape[-1]
    groups = lax.axis_size("slc")
    spread = max(1, per_device // groups)
    slot_count = groups * spread
    cos_table, sin_table = fourier_tables(matrix)
    section_one = jnp.stack([jnp.stack([cos_table, -sin_table]), jnp.stack([sin_table, cos_table])])
    section_two = jnp.stack([jnp.stack([cos_table, sin_table]), jnp.stack([-sin_table, cos_table])])
    image_re = images[:, None, :, 0].astype(jnp.float32)
    image_im = images[:, None, :, 1].astype(jnp.float32)
    map_re = coil_maps[None, :, :, 0].astype(jnp.float32)
    map_im = coil_maps[None, :, :, 1].astype(jnp.float32)
    coil_image = jnp.stack(
        [map_re * image_re - map_im * image_im, map_re * image_im + map_im * image_re], axis=3
    ).astype(jnp.bfloat16)
    partly = jnp.einsum(
        "pqky,tcsqyx->tcspkx", section_one, coil_image, preferred_element_type=jnp.float32
    ).astype(jnp.bfloat16)
    spectra = jnp.einsum(
        "tcsqyx,qpkx->tcspyk", partly, section_two, preferred_element_type=jnp.float32
    )
    phase_angle = slice_phases(shift_index, phase_offset, matrix)
    cosine = jnp.cos(phase_angle)[None, None, :, :, None]
    sine = jnp.sin(phase_angle)[None, None, :, :, None]
    spec_re = spectra[:, :, :, 0]
    spec_im = spectra[:, :, :, 1]
    shifted = jnp.stack(
        [spec_re * cosine - spec_im * sine, spec_re * sine + spec_im * cosine], axis=3
    ).astype(jnp.bfloat16)
    position = lax.axis_index("slc")
    within = jnp.arange(per_device, dtype=jnp.int32)
    classes = (position * per_device + within) % groups
    class_match = (classes[:, None] == jnp.arange(groups, dtype=jnp.int32)[None, :]).astype(
        jnp.int32
    )
    target = jnp.sum(class_match * group_order[None, :], axis=1)
    slot_index = target * spread + within // groups
    onehot = (jnp.arange(slot_count, dtype=jnp.int32)[:, None] == slot_index[None, :]).astype(
        jnp.int32
    )
    source = jnp.sum(onehot * within[None, :], axis=1)
    filled = jnp.sum(onehot, axis=1)
    outgoing = jnp.take(shifted, source, axis=2)
    outgoing = jnp.where(
        filled[None, None, :, None, None, None] > 0, outgoing, jnp.zeros_like(outgoing)
    )
    incoming = lax.all_to_all(outgoing, "slc", split_axis=2, concat_axis=2, tiled=True)
    aliased = jnp.sum(incoming, axis=2, dtype=jnp.float32)
    residual = (aliased - kspace[:, 0].astype(jnp.float32)).astype(jnp.bfloat16)
    partial_value = jnp.einsum(
        "tcpyx,tcyx->py",
        incoming[:, :, :, 0],
        residual[:, :, 1],
        preferred_element_type=jnp.float32,
    )
    partial_value = partial_value - jnp.einsum(
        "tcpyx,tcyx->py",
        incoming[:, :, :, 1],
        residual[:, :, 0],
        preferred_element_type=jnp.float32,
    )
    returned = lax.all_to_all(partial_value, "slc", split_axis=0, concat_axis=0, tiled=True)
    local_grad = jnp.dot(onehot.T.astype(jnp.float32), returned, precision=lax.Precision.HIGHEST)
    summed = lax.psum(local_grad, "coil")
    summed = lax.psum(summed, "vol")
    factor = 1.0 / (
        coil_maps.shape[0] * lax.axis_size("coil") * images.shape[0] * lax.axis_size("vol")
    )
    return summed * factor


def solution(mesh):
    placed = (
        P(("grp", "vol"), "slc", None, None, None),
        P(("grp", "coil"), "slc", None, None, None),
        P(("grp", "vol"), "slc", "coil", None, None, None),
        P("slc"),
        P("slc", None),
        P(),
    )
    return jax.shard_map(
        program, mesh=mesh, in_specs=placed, out_specs=P(("grp", "slc"), None), check_vma=False
    )
```
